32 devices in a mesh: dp: 8 (over z, x), mp: 4 (over y, core).
Axes of the slice: x: 2, y: 2, z: 4, core: 2. Of those that a mesh axis runs over, the one named last changes fastest.
Arguments:
- block_input: bfloat16 [8, 1024, 1024], P('dp', 'mp'), may hold values from -6 to 6
- out_grad: bfloat16 [8, 1024, 1024], P('dp', 'mp'), may hold values from -6 to 6
- lengths: int32 [8], P('dp'), may hold values from 256 to 1024, as said below
- owner: int32 [48], replicated, may hold values from 0 to 47, as said below
- gain_one: float32 [1024], replicated, may hold values from 0.5 to 1.5
- shift_one: float32 [1024], replicated, may hold values from -3 to 3
- gain_two: float32 [1024], replicated, may hold values from 0.5 to 1.5
- shift_two: float32 [1024], replicated, may hold values from -3 to 3
- master: float32 [48, 4, 256, 256], P('dp', 'mp'), as said below
- moment_one: float32 [48, 4, 256, 256], P('dp', 'mp'), may hold values from -112 to 112
- moment_two: float32 [48, 4, 256, 256], P('dp', 'mp'), may hold values from 81.92 to 819.2
- left_basis: float32 [48, 4, 256, 256], P('dp', 'mp'), may hold values from -0.375 to 0.375
- right_basis: float32 [48, 4, 256, 256], P('dp', 'mp'), may hold values from -0.375 to 0.375
Outputs:
- block_output: bfloat16 [8, 1024, 1024], P('dp', 'mp')
- input_grad: float32 [8, 1024, 1024], P('dp', 'mp')
- norm_grads: float32 [4, 1024], replicated
- weight_grads: float32 [48, 4, 256, 256], P('dp', 'mp')
- moment_one_new: float32 [48, 4, 256, 256], P('dp', 'mp')
- moment_two_new: float32 [48, 4, 256, 256], P('dp', 'mp')
- weight_update: float32 [48, 4, 256, 256], P('dp', 'mp')
- weight_copy: bfloat16 [48, 4, 256, 256], P('dp', 'mp')
- head_clip: float32 [16], P('mp')
The draws below stay inside these ranges and needn't reach their ends.
Inputs may be any that keep to these rules, and one draw needn't show every extreme that they name: The 8 lengths are 256 + (768 * r) // 7 for r = 0 .. 7, each once, in drawn order. `owner`: distinct slots; slot s lies on index s // 6 of dp; slots 0 and 47 always own a tile. `master`: slot owner[t] holds tile t; slots that own no tile are not read.
All inputs are finite; a program needn't handle non-finite values.
Results may differ from the reference program's by a relative error of at most 0.012.
The reference program's roundings to bfloat16 on the way count: a program that leaves them out, or rounds other values in their place, can miss the bound.
Values may be sent and summed in bfloat16 or wider, within the bound.
No kernel may reach another device: no remote copies, remote signals or barrier semaphores. Data moves between devices by JAX's collectives and lax.ppermute only.
A program may use at most 192 MiB of HBM per device.

```python
import math
import jax
import jax.numpy as jnp
from jax import lax

D = 1024
HEADS = 16
ROT = 16
FF = 4096
TILE = 256
LEN = 1024
SEQS = 8
TILES = 48
SLOT_ALL = 48
N_MP = 4


def owner_slots(key):
    base = jax.random.fold_in(key, 7001)
    first_key, second_key = jax.random.split(base)
    middle = jax.random.permutation(first_key, SLOT_ALL - 2).astype(jnp.int32) + 1
    ends = jnp.array([0, SLOT_ALL - 1], dtype=jnp.int32)
    chosen = jnp.concatenate([ends, middle[:TILES - 2]])
    return jax.random.permutation(second_key, chosen).astype(jnp.int32)


def draw_owner(key, part):
    return owner_slots(key)


def draw_lengths(key, part):
    order = jax.random.permutation(jax.random.fold_in(key, 7002), SEQS).astype(jnp.int32)
    return (LEN // 4 + (LEN - LEN // 4) * order // (SEQS - 1)).astype(jnp.int32)


def draw_master(key, part):
    owner = owner_slots(key)
    slot_ids = jnp.arange(SLOT_ALL, dtype=jnp.int32)
    match = owner[None, :] == slot_ids[:, None]
    tile_of = jnp.sum(jnp.where(match, jnp.arange(TILES, dtype=jnp.int32)[None, :], 0), axis=1)
    narrow_blocks = D // N_MP // TILE
    row_blocks = D // TILE
    unit_blocks = FF // N_MP // TILE
    count_mix = 3 * row_blocks * narrow_blocks
    count_out = narrow_blocks * row_blocks
    count_up = row_blocks * unit_blocks
    base_scale = jnp.where(tile_of < count_mix, D ** (-0.5), jnp.where(tile_of < count_mix + count_out, 8.0 * D ** (-0.5), jnp.where(tile_of < count_mix + count_out + count_up, D ** (-0.5), FF ** (-0.5)))).astype(jnp.float32)
    head_gain = jax.random.uniform(jax.random.fold_in(key, 7003), (HEADS,), jnp.float32, 1.0, 1.7)
    per_part = HEADS // N_MP
    head_size = D // HEADS
    column_head = ((tile_of % narrow_blocks)[:, None, None] * TILE + jnp.arange(TILE, dtype=jnp.int32)[None, None, :]) // head_size
    head_index = jnp.arange(N_MP, dtype=jnp.int32)[None, :, None] * per_part + column_head
    column_gain = jnp.where((tile_of < 2 * row_blocks * narrow_blocks)[:, None, None], head_gain[head_index], 1.0)
    noise_key = jax.random.fold_in(key, 7005)
    shape = (SLOT_ALL, N_MP, TILE, TILE)
    noise = jax.random.normal(noise_key, shape, jnp.float32)
    return noise * base_scale[:, None, None, None] * column_gain[:, :, None, :]


def level_of(stream_key, dims, cuts, low, largest):
    factor_of = 1.0
    for axis_at, parts in cuts:
        heights = jax.random.uniform(jax.random.fold_in(jax.random.fold_in(stream_key, 6), axis_at), (parts,), jnp.float32, low / len(cuts), largest / len(cuts))
        factor_of = factor_of * jnp.repeat(jnp.exp(heights), dims[axis_at] // parts).reshape((-1,) + (1,) * (len(dims) - 1 - axis_at))
    return factor_of


def gaussian(stream_key, extent, spread, most, cuts=(), kind=jnp.bfloat16):
    level = level_of(stream_key, extent, cuts, -0.22, 0.18) if cuts else 1.0
    entries = jax.random.normal(stream_key, extent, jnp.float32) * spread * level
    return jnp.minimum(jnp.maximum(entries, -most), most).astype(kind)


def setup_inputs(seed: int = 0) -> dict:
    streams_of = jax.random.split(jax.random.key(seed), 14)
    block_input = gaussian(streams_of[0], (SEQS, LEN, D), 1.0, 6.0, ((0, 8), (1, 4)))
    out_grad = gaussian(streams_of[1], (SEQS, LEN, D), 1.0, 6.0, ((0, 8), (1, 4)))
    lengths = draw_lengths(jax.random.fold_in(streams_of[13], 71), 0)
    owner = draw_owner(jax.random.fold_in(streams_of[13], 71), 0)
    gain_one = jnp.clip(1.0 + 0.1 * jax.random.normal(streams_of[4], (D,), jnp.float32), 0.5, 1.5)
    shift_one = gaussian(streams_of[5], (D,), 0.3, 3.0, (), jnp.float32)
    gain_two = jnp.clip(1.0 + 0.1 * jax.random.normal(streams_of[6], (D,), jnp.float32), 0.5, 1.5)
    shift_two = gaussian(streams_of[7], (D,), 0.3, 3.0, (), jnp.float32)
    master = draw_master(jax.random.fold_in(streams_of[13], 71), 0)
    moment_one = gaussian(streams_of[9], (SLOT_ALL, N_MP, TILE, TILE), (0.2 * (LEN * SEQS) ** 0.5), 112.0, ((0, 8), (1, 4)), jnp.float32)
    moment_two = jnp.clip(jnp.exp(math.log(819.2) - 2.3025851 * jax.random.uniform(streams_of[10], (SLOT_ALL, N_MP, TILE, TILE), jnp.float32) ** level_of(streams_of[10], (SLOT_ALL, N_MP, TILE, TILE), ((0, 8), (1, 4)), -0.2, 0.2)), 81.92, 819.2)
    left_basis = gaussian(streams_of[11], (SLOT_ALL, N_MP, TILE, TILE), TILE ** -0.5, 0.375, ((0, 8), (1, 4)), jnp.float32)
    right_basis = gaussian(streams_of[12], (SLOT_ALL, N_MP, TILE, TILE), TILE ** -0.5, 0.375, ((0, 8), (1, 4)), jnp.float32)
    return {"block_input": block_input, "out_grad": out_grad, "lengths": lengths, "owner": owner, "gain_one": gain_one, "shift_one": shift_one, "gain_two": gain_two, "shift_two": shift_two, "master": master, "moment_one": moment_one, "moment_two": moment_two, "left_basis": left_basis, "right_basis": right_basis}


@jax.custom_vjp
def low(v):
    return lax.optimization_barrier(v.astype(jnp.bfloat16)).astype(jnp.float32)

@jax.custom_vjp
def low_back(v):
    return v

def low_keep(v):
    return (low(v), None)

def low_pass(kept, grad):
    return (grad,)

def back_keep(v):
    return (v, None)

def back_low(kept, grad):
    return (low(grad),)
low.defvjp(low_keep, low_pass)
low_back.defvjp(back_keep, back_low)
exact = lax.Precision.HIGHEST
norm_eps = 1e-05
clip_tau = 8.0
step_rate = 0.03
adam_eps = 1e-08
masked_fill = -1e+30

def tile_column(part_mix, part_out, part_up, part_down, size):
    model = part_mix.shape[0]
    narrow = part_mix.shape[2]
    units_here = part_up.shape[1]
    first_tiles = part_mix.reshape(model // size, size, 3, narrow // size, size).transpose(2, 0, 3, 1, 4).reshape(-1, size, size)
    second_tiles = part_out.reshape(narrow // size, size, model // size, size).transpose(0, 2, 1, 3).reshape(-1, size, size)
    third_tiles = part_up.reshape(model // size, size, units_here // size, size).transpose(0, 2, 1, 3).reshape(-1, size, size)
    fourth_tiles = part_down.reshape(units_here // size, size, model // size, size).transpose(0, 2, 1, 3).reshape(-1, size, size)
    return jnp.concatenate([first_tiles, second_tiles, third_tiles, fourth_tiles], axis=0)

def untile_column(tiles, model, narrow, units_here):
    size = tiles.shape[-1]
    row_blocks = model // size
    narrow_blocks = narrow // size
    unit_blocks = units_here // size
    count_mix = 3 * row_blocks * narrow_blocks
    count_out = narrow_blocks * row_blocks
    count_up = row_blocks * unit_blocks
    part_mix = tiles[:count_mix].reshape(3, row_blocks, narrow_blocks, size, size).transpose(1, 3, 0, 2, 4).reshape(model, 3, narrow)
    part_out = tiles[count_mix:count_mix + count_out].reshape(narrow_blocks, row_blocks, size, size).transpose(0, 2, 1, 3).reshape(narrow, model)
    part_up = tiles[count_mix + count_out:count_mix + count_out + count_up].reshape(row_blocks, unit_blocks, size, size).transpose(0, 2, 1, 3).reshape(model, units_here)
    part_down = tiles[count_mix + count_out + count_up:].reshape(unit_blocks, row_blocks, size, size).transpose(0, 2, 1, 3).reshape(units_here, model)
    return (part_mix, part_out, part_up, part_down)

def normalize(values, gain, shift):
    centered = values - lax.optimization_barrier(jnp.mean(values, axis=-1, keepdims=True))
    inverse_root = lax.rsqrt(lax.optimization_barrier(jnp.mean(centered * centered, axis=-1, keepdims=True)) + norm_eps)
    return centered * inverse_root * gain + shift

def rotary_tables(length):
    half = ROT // 2
    inverse = 10000.0 ** (-(2.0 * jnp.arange(half, dtype=jnp.float32)) / ROT)
    angles = jnp.arange(length, dtype=jnp.float32)[:, None] * inverse[None, :]
    return (jnp.cos(angles), jnp.sin(angles))

def rotate(values, cosine, sine):
    half = ROT // 2
    lower = values[..., :half]
    upper = values[..., half:ROT]
    cos_rows = cosine[:, None, :]
    sin_rows = sine[:, None, :]
    return jnp.concatenate([lower * cos_rows - upper * sin_rows, upper * cos_rows + lower * sin_rows, values[..., ROT:]], axis=-1)

def attend(query, keys, values, length):
    total_rows = query.shape[0]
    block_rows = min(512, total_rows)
    block_count = total_rows // block_rows
    heads = query.shape[1]
    scale = query.shape[2] ** (-0.5)
    positions = jnp.arange(total_rows, dtype=jnp.int32)

    def block(pieces):
        q_rows, start = pieces
        rows_pos = start + jnp.arange(block_rows, dtype=jnp.int32)
        scores = low_back(jnp.einsum('qhe,khe->hqk', q_rows, keys, precision=exact) * scale)
        allowed = (positions[None, :] <= rows_pos[:, None]) & (positions[None, :] < length)
        masked = jnp.where(allowed[None], scores, masked_fill)
        peak = lax.optimization_barrier(jnp.max(masked, axis=-1, keepdims=True))
        expo = jnp.exp(masked - peak)
        prob = low(expo / lax.optimization_barrier(jnp.sum(expo, axis=-1, keepdims=True)))
        result = jnp.einsum('hqk,khe->qhe', prob, values, precision=exact)
        counted = allowed & (rows_pos < length)[:, None]
        top = lax.optimization_barrier(jnp.max(jnp.where(counted[None], scores, masked_fill), axis=(1, 2)))
        return (result, top)
    starts = jnp.arange(block_count, dtype=jnp.int32) * block_rows
    results, tops = lax.map(jax.checkpoint(block), (query.reshape(block_count, block_rows, heads, -1), starts))
    return (results.reshape(total_rows, heads, -1), lax.optimization_barrier(jnp.max(tops, axis=0)))

def reference(block_input, out_grad, lengths, owner, gain_one, shift_one, gain_two, shift_two, master, moment_one, moment_two, left_basis, right_basis):
    narrow = D // N_MP
    units_here = FF // N_MP
    head_size = D // HEADS
    owned = low(master)[owner]
    columns = [untile_column(owned[:, part], D, narrow, units_here) for part in range(N_MP)]
    mix_weight = jnp.concatenate([column[0] for column in columns], axis=2)
    out_weight = jnp.concatenate([column[1] for column in columns], axis=0)
    up_weight = jnp.concatenate([column[2] for column in columns], axis=1)
    down_weight = jnp.concatenate([column[3] for column in columns], axis=0)
    cosine, sine = rotary_tables(LEN)

    def one_sequence(params, x_seq, length):
        gain_a, shift_a, gain_b, shift_b, mix_w, out_w, up_w, down_w = params
        xn_one = low(normalize(x_seq, gain_a, shift_a))
        xn_two = low(normalize(x_seq, gain_b, shift_b))
        mixed = low_back(jnp.dot(xn_one, mix_w.reshape(D, 3 * D), precision=exact)).reshape(LEN, 3, HEADS, head_size)
        query = low(rotate(mixed[:, 0], cosine, sine))
        keys = low(rotate(mixed[:, 1], cosine, sine))
        values = low(mixed[:, 2])
        attended, tops = attend(query, keys, values, length)
        joined = low_back(low(attended.reshape(LEN, D)))
        hidden = low_back(jnp.dot(xn_two, up_w, precision=exact))
        active = low(jax.nn.gelu(hidden, approximate=False))
        result = x_seq + jnp.dot(joined, out_w, precision=exact) + jnp.dot(active, down_w, precision=exact)
        return (result, tops)
    group = min(SEQS, max(1, 4096 // LEN))
    while SEQS % group != 0:
        group = group - 1

    def forward(params, inputs):
        grouped = inputs.reshape(SEQS // group, group, LEN, D)
        grouped_len = lengths.reshape(SEQS // group, group)

        def step_fn(carry, pieces):
            results, tops = jax.vmap(one_sequence, in_axes=(None, 0, 0))(params, pieces[0], pieces[1])
            return (jnp.maximum(carry, lax.optimization_barrier(jnp.max(tops, axis=0))), results)
        start_max = jnp.full((HEADS,), masked_fill, dtype=jnp.float32)
        peaks, results = lax.scan(jax.checkpoint(step_fn), start_max, (grouped, grouped_len))
        return (results.reshape(SEQS, LEN, D), peaks)
    params = (gain_one, shift_one, gain_two, shift_two, mix_weight, out_weight, up_weight, down_weight)
    inputs = block_input.astype(jnp.float32)
    outputs, pullback, peaks = jax.vjp(forward, params, inputs, has_aux=True)
    valid = jnp.arange(LEN, dtype=jnp.int32)[None, :] < lengths[:, None]
    cot = jnp.where(valid[:, :, None], out_grad.astype(jnp.float32), jnp.zeros((), jnp.float32))
    grads, input_grad = pullback(cot)
    norm_grads = jnp.stack([grads[0], grads[1], grads[2], grads[3]])
    grad_mix, grad_out, grad_up, grad_down = (grads[4], grads[5], grads[6], grads[7])
    tiled = jnp.stack([tile_column(grad_mix[:, :, part * narrow:(part + 1) * narrow], grad_out[part * narrow:(part + 1) * narrow], grad_up[:, part * units_here:(part + 1) * units_here], grad_down[part * units_here:(part + 1) * units_here], TILE) for part in range(N_MP)], axis=1)
    weight_grads = jnp.zeros((SLOT_ALL, N_MP, TILE, TILE), jnp.float32).at[owner].set(tiled)
    live = jnp.zeros((SLOT_ALL,), jnp.float32).at[owner].set(1.0)
    tile_of = jnp.zeros((SLOT_ALL,), jnp.int32).at[owner].set(jnp.arange(TILES, dtype=jnp.int32))
    partial_rot = jnp.einsum('spba,spbc->spac', left_basis, weight_grads, precision=exact)
    rotated = jnp.einsum('spac,spcd->spad', partial_rot, right_basis, precision=exact)
    live_tiles = live[:, None, None, None]
    moment_one_new = (0.5 * moment_one + 0.5 * rotated) * live_tiles
    moment_two_new = (0.5 * moment_two + 0.5 * rotated * rotated) * live_tiles
    normed_step = moment_one_new / (jnp.sqrt(moment_two_new) + adam_eps)
    partial_back = jnp.einsum('spab,spbc->spac', left_basis, normed_step, precision=exact)
    step = jnp.einsum('spac,spdc->spad', partial_back, right_basis, precision=exact)
    narrow_blocks = narrow // TILE
    column_head = ((tile_of % narrow_blocks)[:, None, None] * TILE + jnp.arange(TILE, dtype=jnp.int32)[None, None, :]) // head_size
    head_index = jnp.arange(N_MP, dtype=jnp.int32)[None, :, None] * (HEADS // N_MP) + column_head
    head_clip = clip_tau / jnp.maximum(peaks, clip_tau)
    is_query_key = tile_of < 2 * (D // TILE) * narrow_blocks
    column_scale = jnp.where(is_query_key[:, None, None], jnp.sqrt(head_clip[head_index]), jnp.ones((), jnp.float32))
    new_master = (master - step_rate * step) * column_scale[:, :, None, :] * live_tiles
    weight_update = new_master - master * live_tiles
    return (outputs.astype(jnp.bfloat16), input_grad, norm_grads, weight_grads, moment_one_new, moment_two_new, weight_update, new_master.astype(jnp.bfloat16), head_clip)
```

```python
import functools
import jax
import jax.numpy as jnp
from jax import lax
from jax.experimental import pallas as pl
from jax.experimental.pallas import tpu as pltpu
from jax.sharding import PartitionSpec as P

HEADS = 16
ROT = 16
FF = 4096

norm_eps = 1e-05
clip_tau = 8.0
step_rate = 0.03
adam_eps = 1e-08
masked_fill = -1e30
f32 = jnp.float32
bf16 = jnp.bfloat16
VM = pltpu.VMEM
ANY = pl.ANY


def dot_nn(a, b):
    return lax.dot_general(a, b, (((1,), (0,)), ((), ())), preferred_element_type=f32)


def dot_nt(a, b):
    return lax.dot_general(a, b, (((1,), (1,)), ((), ())), preferred_element_type=f32)


def normed_rows(x):
    centered = x - jnp.mean(x, axis=-1, keepdims=True)
    inverse = lax.rsqrt(jnp.mean(centered * centered, axis=-1, keepdims=True) + norm_eps)
    return centered * inverse, inverse


def norm_body(groups, info, affine, *refs):
    xs = refs[:groups]
    cs = refs[groups : 2 * groups]
    xn1, xn2, xn1t, xn2t, cot, xall = refs[2 * groups :]
    rows, model = xs[0].shape
    step = 32
    block = 256
    place = info[0]
    length = info[1]
    for i in range(groups):
        base = (place ^ i) * rows

        def chunk(c, carry, i=i, base=base):
            r = pl.multiple_of(c * step, step)
            at = pl.ds(pl.multiple_of(base + r, step), step)
            raw = xs[i][pl.ds(r, step), :]
            normed, _ = normed_rows(raw.astype(f32))
            xall[at, :] = raw
            xn1[at, :] = (normed * affine[0:1, :] + affine[1:2, :]).astype(bf16)
            xn2[at, :] = (normed * affine[2:3, :] + affine[3:4, :]).astype(bf16)
            pos = base + r + lax.broadcasted_iota(jnp.int32, (step, 1), 0)
            cot[at, :] = jnp.where(pos < length, cs[i][pl.ds(r, step), :].astype(f32), 0.0).astype(bf16)
            return carry

        lax.fori_loop(0, rows // step, chunk, 0)

        def flip(c, carry, base=base):
            col = pl.ds(pl.multiple_of(c * block, block), block)
            row = pl.ds(pl.multiple_of(base, rows), rows)
            xn1t[col, row] = xn1[row, col].T
            xn2t[col, row] = xn2[row, col].T
            return carry

        lax.fori_loop(0, model // block, flip, 0)


def norm_call(groups, info, affine, xs, cs):
    rows, model = xs[0].shape
    total = rows * groups
    shape = jax.ShapeDtypeStruct((total, model), bf16)
    shape_t = jax.ShapeDtypeStruct((model, total), bf16)
    v = pl.BlockSpec(memory_space=VM)
    return pl.pallas_call(
        functools.partial(norm_body, groups),
        out_shape=(shape, shape, shape_t, shape_t, shape, shape),
        in_specs=[pl.BlockSpec(memory_space=pltpu.SMEM)] + [v] * (1 + 2 * groups),
        out_specs=(v,) * 6,
        name="norms",
    )(info, affine, *xs, *cs)


def mlp_body(layout, counts, tab, xn2, xn2t, cot, *refs):
    n = len(counts)
    bufs = refs[:n]
    act, hg, grads, wout, wv, actt, sem_in, sem_out = refs[n:]
    rbs, ubs, up0, down0, tile_count, size = layout
    tokens = xn2.shape[0]
    e = 0
    for b in range(n):
        for j in range(counts[b]):
            t = tab[e]

            @pl.when(t >= 0)
            def _(b=b, j=j, t=t):
                pltpu.make_async_copy(bufs[b].at[j], wv.at[t], sem_in.at[t]).start()

            e += 1

    def arrived(t):
        pltpu.make_async_copy(bufs[0].at[0], wv.at[t], sem_in.at[t]).wait()

    def arrive(t, carry):
        arrived(t)
        return carry

    lax.fori_loop(up0, tile_count, arrive, 0)

    blocks = tokens // size

    def token_block(m, carry):
        row = pl.ds(pl.multiple_of(m * size, size), size)
        for ub in range(ubs):
            col = slice(ub * size, (ub + 1) * size)
            h = dot_nn(xn2[row, 0:size], wv[up0 + ub])
            for rb in range(1, rbs):
                h += dot_nn(xn2[row, rb * size : (rb + 1) * size], wv[up0 + rb * ubs + ub])
            ag = dot_nt(cot[row, 0:size], wv[down0 + ub * rbs])
            for rb in range(1, rbs):
                ag += dot_nt(cot[row, rb * size : (rb + 1) * size], wv[down0 + ub * rbs + rb])
            cumulative = 0.5 * (1.0 + lax.erf(h * 0.7071067811865476))
            density = 0.3989422804014327 * jnp.exp(-0.5 * h * h)
            a = (h * cumulative).astype(bf16)
            act[row, col] = a
            actt[col, row] = a.T
            hg[row, col] = (ag * (cumulative + h * density)).astype(bf16)
        return carry

    lax.fori_loop(0, blocks, token_block, 0)

    def unit_block(ub, carry):
        col = pl.ds(pl.multiple_of(ub * size, size), size)
        for rb in range(rbs):
            at = slice(rb * size, (rb + 1) * size)
            grads[rb * ubs + ub] = dot_nn(xn2t[at, :], hg[:, col]).astype(bf16)
            grads[rbs * ubs + ub * rbs + rb] = dot_nn(actt[col, :], cot[:, at]).astype(bf16)
        return carry

    lax.fori_loop(0, ubs, unit_block, 0)
    lax.fori_loop(0, up0, arrive, 0)
    out = pltpu.make_async_copy(wv, wout, sem_out)
    out.start()
    out.wait()


def mlp_call(layout, tab, xn2, xn2t, cot, bufs):
    rbs, ubs, up0, down0, tile_count, size = layout
    tokens = xn2.shape[0]
    units = ubs * size
    counts = tuple(b.shape[0] for b in bufs)
    v = pl.BlockSpec(memory_space=VM)
    anyspec = pl.BlockSpec(memory_space=ANY)
    return pl.pallas_call(
        functools.partial(mlp_body, layout, counts),
        out_shape=(
            jax.ShapeDtypeStruct((tokens, units), bf16),
            jax.ShapeDtypeStruct((tokens, units), bf16),
            jax.ShapeDtypeStruct((2 * rbs * ubs, size, size), bf16),
            jax.ShapeDtypeStruct((tile_count, size, size), bf16),
        ),
        in_specs=[pl.BlockSpec(memory_space=pltpu.SMEM), v, v, v] + [anyspec] * len(bufs),
        out_specs=(v, v, v, anyspec),
        scratch_shapes=[
            VM((tile_count, size, size), bf16),
            VM((units, tokens), bf16),
            pltpu.SemaphoreType.DMA((tile_count,)),
            pltpu.SemaphoreType.DMA,
        ],
        name="feed_forward",
    )(tab, xn2, xn2t, cot, *bufs)


def swap_halves(x, heads, head_size):
    half = ROT // 2
    lane = lax.broadcasted_iota(jnp.int32, x.shape, 1) % head_size
    down = pltpu.roll(x, x.shape[1] - half, 1)
    up = pltpu.roll(x, half, 1)
    return jnp.where(lane < half, down, up)


def attn_body(layout, info, xn1, cot, w, cosf, sinf, cost, sint, mg, att, attt, tops,
              q, k, v, vt, kt, do, dqt, dk, dv):
    rbs, heads, head_size, size, mix_tiles, scale = layout
    tokens = xn1.shape[0]
    width = heads * head_size
    blocks = tokens // size
    half = ROT // 2
    length = info[1]

    def project(m, carry):
        row = pl.ds(pl.multiple_of(m * size, size), size)
        for c in range(3):
            acc = dot_nn(xn1[row, 0:size], w[c * rbs])
            for rb in range(1, rbs):
                acc += dot_nn(xn1[row, rb * size : (rb + 1) * size], w[c * rbs + rb])
            if c < 2:
                acc = acc * cosf[row, :] + swap_halves(acc, heads, head_size) * sinf[row, :]
            low = acc.astype(bf16)
            if c == 0:
                q[row, :] = low * bf16(scale)
            elif c == 1:
                k[row, :] = low
                kt[:, row] = low.T
            else:
                v[row, :] = low
                vt[:, row] = low.T
        acc = dot_nt(cot[row, 0:size], w[mix_tiles])
        for rb in range(1, rbs):
            acc += dot_nt(cot[row, rb * size : (rb + 1) * size], w[mix_tiles + rb])
        do[row, :] = acc.astype(bf16)
        return carry

    lax.fori_loop(0, blocks, project, 0)
    dk[...] = jnp.zeros_like(dk)
    dv[...] = jnp.zeros_like(dv)
    lane128 = lax.broadcasted_iota(jnp.int32, (8, 128), 1)
    top = jnp.full((8, 128), masked_fill, f32)
    for i in range(blocks):
        reach = (i + 1) * size
        at = slice(i * size, (i + 1) * size)
        key_pos = lax.broadcasted_iota(jnp.int32, (reach, size), 0)
        row_pos = i * size + lax.broadcasted_iota(jnp.int32, (reach, size), 1)
        lane_head = lax.broadcasted_iota(jnp.int32, (size, width), 1) // head_size

        def one_head(h, top, i=i, reach=reach, at=at, key_pos=key_pos, row_pos=row_pos,
                     lane_head=lane_head):
            mine = lane_head == h
            hrow = pl.ds(pl.multiple_of(h * head_size, head_size), head_size)
            qh = jnp.where(mine, q[at, :], jnp.zeros((), bf16))
            doh = jnp.where(mine, do[at, :], jnp.zeros((), bf16))
            s = dot_nt(k[0:reach, :], qh)
            dp = dot_nt(v[0:reach, :], doh)
            allowed = (key_pos <= row_pos) & (key_pos < length)
            s = jnp.where(allowed, s, masked_fill)
            m = jnp.max(s, axis=0, keepdims=True)
            e = jnp.exp(s - m)
            p = e * (1.0 / jnp.sum(e, axis=0, keepdims=True))
            pb = p.astype(bf16)
            inner = jnp.sum(p * dp, axis=0, keepdims=True)
            ds = (p * (dp - inner)).astype(bf16)
            attt[hrow, at] = dot_nn(vt[hrow, 0:reach], pb).astype(bf16)
            dqt[hrow, at] = dot_nn(kt[hrow, 0:reach], ds) * scale
            dv[0:reach, :] += dot_nn(pb, doh)
            dk[0:reach, :] += dot_nn(ds, qh)
            seen = jnp.where(row_pos[0:1, :] < length, m, masked_fill)
            best = jnp.max(seen, axis=1, keepdims=True)
            return jnp.where(lane128 == h, jnp.maximum(top, best), top)

        top = lax.fori_loop(0, heads, one_head, top)
    tops[...] = top

    for h in range(heads):
        lo = slice(h * head_size, h * head_size + half)
        hi = slice(h * head_size + half, h * head_size + ROT)
        a = dqt[lo, :]
        b = dqt[hi, :]
        dqt[lo, :] = a * cost[...] + b * sint[...]
        dqt[hi, :] = b * cost[...] - a * sint[...]

    def finish(m, carry):
        row = pl.ds(pl.multiple_of(m * size, size), size)
        mg[row, 0:width] = dqt[:, row].astype(bf16).T
        g = dk[row, :]
        g = g * cosf[row, :] - swap_halves(g, heads, head_size) * sinf[row, :]
        mg[row, width : 2 * width] = g.astype(bf16)
        mg[row, 2 * width : 3 * width] = dv[row, :].astype(bf16)
        att[row, :] = attt[:, row].T
        return carry

    lax.fori_loop(0, blocks, finish, 0)


def attn_call(layout, info, xn1, cot, w, cosf, sinf, cost, sint):
    rbs, heads, head_size, size, mix_tiles, scale = layout
    tokens = xn1.shape[0]
    width = heads * head_size
    v = pl.BlockSpec(memory_space=VM)
    wide = VM((tokens, width), bf16)
    tall = VM((width, tokens), bf16)
    return pl.pallas_call(
        functools.partial(attn_body, layout),
        out_shape=(
            jax.ShapeDtypeStruct((tokens, 3 * width), bf16),
            jax.ShapeDtypeStruct((tokens, width), bf16),
            jax.ShapeDtypeStruct((width, tokens), bf16),
            jax.ShapeDtypeStruct((8, 128), f32),
        ),
        grid=(1,),
        in_specs=[pl.BlockSpec(memory_space=pltpu.SMEM), v, v,
                  pl.BlockSpec((mix_tiles + rbs, size, size), lambda i: (0, 0, 0)),
                  v, v, v, v],
        out_specs=(v, v, v, v),
        scratch_shapes=[wide, wide, wide, tall, tall, wide, VM((width, tokens), f32),
                        VM((tokens, width), f32), VM((tokens, width), f32)],
        name="attention",
    )(info, xn1, cot, w, cosf, sinf, cost, sint)


def tail_body(layout, counts, info, tab, affine, xall, xn1t, cot, act, hg, mg, att, attt, w, gmlp, *refs):
    rbs, ubs, size, mix_tiles, up0, down0, tile_count, groups = layout
    n = len(counts)
    outs = refs[:n]
    keep, send, nsum, g, sem, sem_g = refs[n:]
    tokens, model = xall.shape
    width = att.shape[1]
    blocks = tokens // size
    place = info[0]
    load = pltpu.make_async_copy(gmlp, g.at[pl.ds(up0, tile_count - up0)], sem_g)
    load.start()
    g[tile_count] = jnp.zeros((size, size), bf16)

    def rb_loop(rb, carry):
        at = pl.ds(pl.multiple_of(rb * size, size), size)
        for c in range(3):
            g[c * rbs + rb] = dot_nn(xn1t[at, :], mg[:, c * width : (c + 1) * width]).astype(bf16)
        g[mix_tiles + rb] = dot_nn(attt[...], cot[:, at]).astype(bf16)
        return carry

    lax.fori_loop(0, rbs, rb_loop, 0)
    load.wait()
    e = 0
    copies = []
    for b in range(n):
        for j in range(counts[b]):
            cp = pltpu.make_async_copy(g.at[tab[e]], outs[b].at[j], sem.at[e])
            cp.start()
            copies.append(cp)
            e += 1
    nsum[...] = jnp.zeros_like(nsum)

    def token_block(m, carry):
        row = pl.ds(pl.multiple_of(m * size, size), size)
        normed, _ = normed_rows(xall[row, :].astype(f32))
        role = place ^ m
        far = role // 2
        near = role % 2 == 0
        for rb in range(rbs):
            at = slice(rb * size, (rb + 1) * size)
            o = dot_nn(att[row, :], w[mix_tiles + rb])
            for ub in range(ubs):
                o += dot_nn(act[row, ub * size : (ub + 1) * size], w[down0 + ub * rbs + rb])
            b1 = dot_nt(mg[row, 0:width], w[rb])
            for c in range(1, 3):
                b1 += dot_nt(mg[row, c * width : (c + 1) * width], w[c * rbs + rb])
            b2 = dot_nt(hg[row, 0:size], w[up0 + rb * ubs])
            for ub in range(1, ubs):
                b2 += dot_nt(hg[row, ub * size : (ub + 1) * size], w[up0 + rb * ubs + ub])
            nm = normed[:, at]
            o = o.astype(bf16)
            b = (b1 * affine[0:1, at] + b2 * affine[2:3, at]).astype(bf16)

            @pl.when(near)
            def _(o=o, b=b, at=at):
                keep[far, 0, :, at] = o
                keep[far, 1, :, at] = b

            @pl.when(jnp.logical_not(near))
            def _(o=o, b=b, at=at):
                send[far, 0, :, at] = o
                send[far, 1, :, at] = b

            nsum[0:1, at] += jnp.sum(b1 * nm, axis=0, keepdims=True)
            nsum[1:2, at] += jnp.sum(b1, axis=0, keepdims=True)
            nsum[2:3, at] += jnp.sum(b2 * nm, axis=0, keepdims=True)
            nsum[3:4, at] += jnp.sum(b2, axis=0, keepdims=True)
        return carry

    lax.fori_loop(0, blocks, token_block, 0)
    for cp in copies:
        cp.wait()


def tail_call(layout, counts, info, tab, affine, xall, xn1t, cot, act, hg, mg, att, attt, w, gmlp):
    rbs, ubs, size, mix_tiles, up0, down0, tile_count, groups = layout
    tokens, model = xall.shape
    assert tokens // groups == size
    s = pl.BlockSpec(memory_space=pltpu.SMEM)
    v = pl.BlockSpec(memory_space=VM)
    anyspec = pl.BlockSpec(memory_space=ANY)
    return pl.pallas_call(
        functools.partial(tail_body, layout, counts),
        out_shape=tuple(jax.ShapeDtypeStruct((c, size, size), bf16) for c in counts)
        + (
            jax.ShapeDtypeStruct((groups // 2, 2, size, model), bf16),
            jax.ShapeDtypeStruct((groups // 2, 2, size, model), bf16),
            jax.ShapeDtypeStruct((8, model), f32),
        ),
        in_specs=[s, s] + [v] * 10 + [anyspec],
        out_specs=(anyspec,) * len(counts) + (v, v, v),
        scratch_shapes=[
            VM((tile_count + 1, size, size), bf16),
            pltpu.SemaphoreType.DMA((sum(counts),)),
            pltpu.SemaphoreType.DMA,
        ],
        name="gradients",
    )(info, tab, affine, xall, xn1t, cot, act, hg, mg, att, attt, w, gmlp)


def split(a):
    hi = a.astype(bf16)
    return hi, (a - hi.astype(f32)).astype(bf16)


def dot3(a, b, dims):
    ah, al = a
    bh, bl = b
    d = lambda x, y: lax.dot_general(x, y, (dims, ((), ())), preferred_element_type=f32)
    return d(ah, bh) + (d(ah, bl) + d(al, bh))


def adam_body(live, col, grad, m1, m2, master, left, right, o_grad, o_m1, o_m2, o_up, o_copy):
    alive = live[pl.program_id(0)]
    ls = split(left[0])
    rs = split(right[0])
    g = grad[0] * alive
    o_grad[0] = g
    partial_rot = dot3(ls, split(g), ((0,), (0,)))
    rotated = dot3(split(partial_rot), rs, ((1,), (0,)))
    first = (0.5 * m1[0] + 0.5 * rotated) * alive
    second = (0.5 * m2[0] + 0.5 * rotated * rotated) * alive
    o_m1[0] = first
    o_m2[0] = second
    norm_step = first / (jnp.sqrt(second) + adam_eps)
    partial_back = dot3(ls, split(norm_step), ((1,), (0,)))
    step = dot3(split(partial_back), rs, ((1,), (1,)))
    new = (master[0] - step_rate * step) * col[0] * alive
    o_up[0] = new - master[0] * alive
    o_copy[0] = new.astype(bf16)


def adam_call(live, col, grad, m1, m2, master, left, right):
    slots, size, _ = grad.shape
    t = pl.BlockSpec((1, size, size), lambda i: (i, 0, 0))
    c = pl.BlockSpec((1, 1, size), lambda i: (i, 0, 0))
    full = jax.ShapeDtypeStruct((slots, size, size), f32)
    return pl.pallas_call(
        adam_body,
        grid=(slots,),
        out_shape=(full, full, full, full, jax.ShapeDtypeStruct((slots, size, size), bf16)),
        in_specs=[pl.BlockSpec(memory_space=pltpu.SMEM), c, t, t, t, t, t, t],
        out_specs=(t,) * 5,
        name="adam",
    )(live, col, grad, m1, m2, master, left, right)


def every_line():
    return range(4)


def z_pairs(moves):
    return [(2 * a + x, 2 * b + x) for a, b in moves for x in range(2)]


def x_pairs(lines):
    return [(2 * z + x, 2 * z + 1 - x) for z in lines for x in range(2)]


pair_moves = [(0, 1), (1, 0), (2, 3), (3, 2)]
middle_moves = [(1, 2), (2, 1)]
outward_moves = [(1, 0), (2, 3)]
inward_moves = [(0, 1), (3, 2)]


def along_dp(value, pairs):
    return lax.ppermute(value, "dp", pairs)


def flip_mp(value, bit, groups):
    return lax.ppermute(value, "mp", [(i, i ^ bit) for i in range(groups)])


def flip_dp(value, bit, wide):
    return lax.ppermute(value, "dp", [(i, i ^ bit) for i in range(wide)])


def far_lines(z):
    middle = (z == 1) | (z == 2)
    a = jnp.where(middle, 3 - z, 3 - (z ^ 1))
    return middle, a, a ^ 1


def line_gather(block):
    r = along_dp(block, z_pairs(pair_moves))
    pa = along_dp(block, z_pairs(middle_moves))
    pb = along_dp(r, z_pairs(middle_moves))
    pc = along_dp(pa, z_pairs(outward_moves))
    pd = along_dp(pb, z_pairs(outward_moves))
    return [block, r, pa, pb, pc, pd]


def grid_gather(copies):
    slots = copies.shape[0]
    cut = max(1, (slots * 5) // 6)
    big = copies[:cut]
    small = copies[cut:]
    pair = jnp.concatenate([small, along_dp(small, x_pairs(range(4)))], axis=0)
    lines = line_gather(big)
    sides = [range(4), range(4), (1, 2), (1, 2), (0, 3), (0, 3)]
    crossed = [along_dp(b, x_pairs(s)) for b, s in zip(lines, sides)]
    pairs = line_gather(pair)
    bufs = lines + crossed + pairs
    here = lax.axis_index("dp")
    z = here // 2
    x = here % 2
    middle, a, b = far_lines(z)
    zs = [z, z ^ 1, a, b, a, b]
    ok = [True, True, middle, middle, ~middle, ~middle]
    ids = []
    for side in (x, 1 - x):
        for zz, good in zip(zs, ok):
            base = (2 * zz + side) * slots + jnp.arange(cut, dtype=jnp.int32)
            ids.append(jnp.where(good, base, -1))
    for zz, good in zip(zs, ok):
        for side in (x, 1 - x):
            base = (2 * zz + side) * slots + jnp.arange(cut, slots, dtype=jnp.int32)
            ids.append(jnp.where(good, base, -1))
    return bufs, jnp.concatenate(ids).astype(jnp.int32)


def grid_scatter_ids(slots):
    cut = max(1, (slots * 5) // 6)
    here = lax.axis_index("dp")
    z = here // 2
    x = here % 2
    _, a, b = far_lines(z)
    zs = [b, a, z ^ 1, z]
    ids = []
    counts = []
    for side in (1 - x, x):
        for zz in zs:
            ids.append((2 * zz + side) * slots + jnp.arange(cut, dtype=jnp.int32))
            counts.append(cut)
    for zz in zs:
        for side in (x, 1 - x):
            ids.append((2 * zz + side) * slots + jnp.arange(cut, slots, dtype=jnp.int32))
        counts.append(2 * (slots - cut))
    return tuple(counts), jnp.concatenate(ids).astype(jnp.int32)


def plus(a, b):
    return a.astype(f32) + b.astype(f32)


def line_reduce(vb, va, vr, vo):
    t1 = along_dp(vb.astype(bf16), z_pairs(inward_moves))
    t3 = along_dp(va.astype(bf16), z_pairs(inward_moves))
    t2 = along_dp(plus(vb, t1).astype(bf16), z_pairs(middle_moves))
    t4 = along_dp(plus(va, t3).astype(bf16), z_pairs(middle_moves))
    t5 = along_dp(plus(vr, t2).astype(bf16), z_pairs(pair_moves))
    return plus(vo, t4) + t5.astype(f32)


def grid_scatter(bufs, slots):
    cut = max(1, (slots * 5) // 6)
    rest = slots - cut
    sent, kept, pairs = bufs[0:4], bufs[4:8], bufs[8:12]
    pair = line_reduce(*pairs)
    crossed = [along_dp(s, x_pairs(range(4))) for s in sent]
    big = line_reduce(*[plus(k, c) for k, c in zip(kept, crossed)])
    small = plus(pair[:rest], along_dp(pair[rest:].astype(bf16), x_pairs(range(4))))
    return jnp.concatenate([big, small], axis=0)


def rope_tables(length, heads, head_size):
    half = ROT // 2
    inverse = 10000.0 ** (-(2.0 * jnp.arange(half, dtype=f32)) / ROT)
    angles = jnp.arange(length, dtype=f32)[:, None] * inverse[None, :]
    c = jnp.cos(angles)
    s = jnp.sin(angles)
    still = jnp.ones((length, head_size - ROT), f32)
    full_c = jnp.tile(jnp.concatenate([c, c, still], 1), (1, heads))
    full_s = jnp.tile(jnp.concatenate([-s, s, jnp.zeros_like(still)], 1), (1, heads))
    return full_c, full_s, c.T, s.T


def local(
    block_input,
    out_grad,
    lengths,
    owner,
    gain_one,
    shift_one,
    gain_two,
    shift_two,
    master,
    moment_one,
    moment_two,
    left_basis,
    right_basis,
):
    groups = lax.axis_size("mp")
    wide = lax.axis_size("dp")
    place = lax.axis_index("mp")
    model = block_input.shape[2]
    rows = block_input.shape[1]
    tokens = rows * groups
    narrow = model // groups
    units = FF // groups
    heads = HEADS // groups
    head_size = model // HEADS
    size = master.shape[-1]
    slots = master.shape[0]
    tile_count = owner.shape[0]
    rbs = model // size
    ubs = units // size
    mix_tiles = 3 * rbs * (narrow // size)
    up0 = mix_tiles + (narrow // size) * rbs
    down0 = up0 + rbs * ubs
    scale = head_size ** (-0.5)
    gridded = wide == 8
    info = jnp.stack([place.astype(jnp.int32), lengths[0]])
    all_slots = jnp.arange(wide * slots, dtype=jnp.int32)
    match = owner[None, :] == all_slots[:, None]
    tile_of = jnp.sum(jnp.where(match, jnp.arange(tile_count, dtype=jnp.int32)[None, :] + 1, 0), axis=1) - 1

    copies = master[:, 0].astype(bf16)
    if gridded:
        weights, ids = grid_gather(copies)
        tab = jnp.where(ids >= 0, tile_of[jnp.maximum(ids, 0)], -1)
    else:
        weights = [lax.all_gather(copies, "dp", axis=0, tiled=True)]
        tab = tile_of

    def spread(v):
        far = flip_mp(v, 2, groups)
        return [v, flip_mp(v, 1, groups), far, flip_mp(far, 1, groups)]

    own_x = block_input[0]
    own_c = out_grad[0]
    affine = jnp.stack([gain_one, shift_one, gain_two, shift_two] * 2)
    xn1, xn2, xn1t, xn2t, cot, xall = norm_call(groups, info, affine, spread(own_x), spread(own_c))
    cosf, sinf, cost, sint = rope_tables(tokens, heads, head_size)
    act, hg, gmlp, w = mlp_call((rbs, ubs, up0, down0, tile_count, size), tab, xn2, xn2t, cot, weights)
    mg, att, attt, tops = attn_call(
        (rbs, heads, head_size, size, mix_tiles, scale), info, xn1, cot, w, cosf, sinf, cost, sint
    )
    peaks = tops
    bit = 1
    while bit < wide:
        peaks = jnp.maximum(peaks, flip_dp(peaks, bit, wide))
        bit *= 2
    if gridded:
        counts, out_ids = grid_scatter_ids(slots)
    else:
        counts, out_ids = (wide * slots,), all_slots
    out_tab = tile_of[out_ids]
    out_tab = jnp.where(out_tab < 0, tile_count, out_tab)
    *shares, keep, send, sums = tail_call(
        (rbs, ubs, size, mix_tiles, up0, down0, tile_count, groups),
        counts, info, out_tab, affine, xall, xn1t, cot, act, hg, mg, att, attt, w, gmlp,
    )
    if gridded:
        mine = grid_scatter(shares, slots)
    else:
        mine = lax.psum_scatter(shares[0].astype(f32), "dp", scatter_dimension=0, tiled=True)

    near = plus(keep, flip_mp(send, 1, groups))
    summed = near[0] + flip_mp(near[1].astype(bf16), 2, groups).astype(f32)
    inputs = own_x.astype(f32)
    normed, inverse = normed_rows(inputs)
    block_output = (inputs + summed[0]).astype(bf16)[None]
    g = summed[1]
    back = inverse * (
        g
        - jnp.mean(g, axis=-1, keepdims=True)
        - normed * jnp.mean(g * normed, axis=-1, keepdims=True)
    )
    local_pos = place * rows + jnp.arange(rows, dtype=jnp.int32)
    cot_here = jnp.where((local_pos < lengths[0])[:, None], own_c.astype(f32), 0.0)
    input_grad = (cot_here + back)[None]

    norm_grads = sums[:4]
    bit = 1
    while bit < groups:
        norm_grads = norm_grads + flip_mp(norm_grads, bit, groups)
        bit *= 2
    bit = 1
    while bit < wide:
        norm_grads = norm_grads + flip_dp(norm_grads, bit, wide)
        bit *= 2

    head_clip = clip_tau / jnp.maximum(peaks[0, :heads], clip_tau)
    mine_ids = lax.axis_index("dp") * slots + jnp.arange(slots, dtype=jnp.int32)
    my_tile = tile_of[mine_ids]
    live = (my_tile >= 0).astype(f32)
    blocks_narrow = narrow // size
    column_head = (
        (my_tile % blocks_narrow)[:, None] * size + jnp.arange(size, dtype=jnp.int32)[None, :]
    ) // head_size
    head_match = column_head[:, :, None] == jnp.arange(heads, dtype=jnp.int32)[None, None, :]
    factor = jnp.sqrt(jnp.sum(jnp.where(head_match, head_clip[None, None, :], 0.0), axis=-1))
    column = jnp.where((my_tile < 2 * rbs * blocks_narrow)[:, None], factor, 1.0)
    grads, first, second, update, copy = adam_call(
        live, column[:, None, :], mine, moment_one[:, 0], moment_two[:, 0], master[:, 0],
        left_basis[:, 0], right_basis[:, 0],
    )
    return (
        block_output,
        input_grad,
        norm_grads,
        grads[:, None],
        first[:, None],
        second[:, None],
        update[:, None],
        copy[:, None],
        head_clip,
    )


def solution(mesh):
    tokens = P("dp", "mp", None)
    tiles = P("dp", "mp", None, None)
    in_specs = (tokens, tokens, P("dp"), P(), P(), P(), P(), P()) + (tiles,) * 5
    out_specs = (tokens, tokens, P()) + (tiles,) * 5 + (P("mp"),)
    return jax.shard_map(local, mesh=mesh, in_specs=in_specs, out_specs=out_specs, check_vma=False)
```
